32 devices in a mesh: user: 4 (over y, x), item: 8 (over z, core).
Axes of the slice: x: 2, y: 2, z: 4, core: 2. Of those that a mesh axis runs over, the one named last changes fastest.
Arguments:
- item_factors: bfloat16 [16384, 256], P('item'), may hold values from -0.125 to 0.125
- item_gram: float32 [256, 256], replicated, as said below
- tile_users: int32 [4, 8, 48], P('user', 'item'), may hold values from 0 to 3
- tile_items: int32 [4, 8, 48], P('user', 'item'), may hold values from 0 to 15, as said below
- tile_counts: int32 [4, 8], P('user', 'item'), may hold values from 12 to 48, as said below
- tile_values: bfloat16 [4, 8, 48, 128, 128], P('user', 'item'), may hold values from 0 to 8
Outputs:
- user_factors: float32 [2048, 256], P(('user', 'item'))
- item_rhs: float32 [8, 2048, 256], P('item', 'user')
The draws below stay inside these ranges and needn't reach their ends.
Inputs may be any that keep to these rules, and one draw needn't show every extreme that they name: `item_gram`: symmetric positive definite. The pairs (tile_users, tile_items) of one device's slots are all different. `tile_counts`: some device uses all 48 slots in every draw.
All inputs are finite; a program needn't handle non-finite values.
Results may differ from the reference program's by a relative error of at most 0.0032.
Values may be sent and summed in bfloat16 or wider, within the bound.
A program may use at most 64 MiB of HBM per device.

```python
import jax
import jax.numpy as jnp
from jax import lax

RANK = 256
TILE = 128
USER_BLK = 4
ITEM_BLK = 16
TILES = 48
ITERS = 3
ITEM_TOTAL = 16384
N_USER = 4
N_ITEM = 8


def draw_item_factors(key, part):
    first, second, third = jax.random.split(jax.random.fold_in(key, 53), 3)
    base = jax.random.normal(first, (ITEM_TOTAL, RANK), jnp.float32) * ITEM_TOTAL ** (-0.5)
    column_slot = jnp.exp(jax.random.uniform(second, (RANK,), jnp.float32, -1.0, 0.5))
    scale_per_row = jnp.exp(jax.random.uniform(third, (ITEM_TOTAL, 1), jnp.float32, jnp.log(0.3), jnp.log(2.0)))
    scale_factor = column_slot[None, :] * scale_per_row / 0.94
    return jnp.clip(base * scale_factor, -0.125, 0.125).astype(jnp.bfloat16)


def draw_item_gram(key, part):
    base = jax.random.normal(key, (RANK, RANK), jnp.float32)
    return 0.5 * jnp.eye(RANK, dtype=jnp.float32) + jnp.dot(base, base.T) / (2 * RANK)


def tile_pairs(key):
    base = jax.random.fold_in(key, 17)
    order = jnp.broadcast_to(jnp.arange(USER_BLK * ITEM_BLK, dtype=jnp.int32), (N_USER * N_ITEM, USER_BLK * ITEM_BLK))
    mixed = jax.random.permutation(base, order, axis=1, independent=True)[:, :TILES]
    return mixed.reshape(N_USER, N_ITEM, TILES).astype(jnp.int32)


def draw_tile_users(key, part):
    return tile_pairs(key) // ITEM_BLK


def draw_tile_items(key, part):
    return tile_pairs(key) % ITEM_BLK


def draw_tile_counts(key, part):
    first, second = jax.random.split(jax.random.fold_in(key, 29))
    ratio = jax.random.randint(first, (N_USER, N_ITEM), 1, 5)
    counts = TILES // ratio
    busiest = jax.random.randint(second, (), 0, N_USER * N_ITEM)
    places = jnp.arange(N_USER * N_ITEM, dtype=jnp.int32).reshape(N_USER, N_ITEM)
    return jnp.where(places == busiest, TILES, counts).astype(jnp.int32)


def draw_tile_values(key, part):
    shape = (N_USER, N_ITEM, TILES, TILE, TILE)
    first, second = jax.random.split(jax.random.fold_in(key, 41))
    keep = jax.random.uniform(first, shape, jnp.float32) < 0.5
    level = jnp.exp(jax.random.uniform(second, shape, jnp.float32, jnp.log(0.5), jnp.log(8.0)))
    return jnp.where(keep, level, 0.0).astype(jnp.bfloat16)


def setup_inputs(seed: int = 0) -> dict:
    arg_keys = jax.random.split(jax.random.key(seed), 7)
    item_factors = draw_item_factors(jax.random.fold_in(arg_keys[6], 71), 0)
    item_gram = draw_item_gram(jax.random.fold_in(arg_keys[6], 71), 0)
    tile_users = draw_tile_users(jax.random.fold_in(arg_keys[6], 71), 0)
    tile_items = draw_tile_items(jax.random.fold_in(arg_keys[6], 71), 0)
    tile_counts = draw_tile_counts(jax.random.fold_in(arg_keys[6], 71), 0)
    tile_values = draw_tile_values(jax.random.fold_in(arg_keys[6], 71), 0)
    return dict(item_factors=item_factors, item_gram=item_gram, tile_users=tile_users, tile_items=tile_items, tile_counts=tile_counts, tile_values=tile_values)


epsilon = 1e-6
highest = lax.Precision.HIGHEST


def confidence_of(tile_vals):
    return jnp.where(tile_vals > 0, 1.0 + tile_vals.astype(jnp.float32), 0.0).astype(jnp.bfloat16)


def chosen_of(block_ids, active, limit):
    return ((block_ids[:, None] == jnp.arange(limit, dtype=jnp.int32)[None, :]) & active[:, None]).astype(jnp.float32)


def reference(item_factors, item_gram, tile_users, tile_items, tile_counts, tile_values):
    block_grid_height = item_factors.reshape(N_ITEM, ITEM_BLK, TILE, RANK)
    active_all = jnp.arange(TILES, dtype=jnp.int32)[None, None, :] < tile_counts[:, :, None]
    group_rows = USER_BLK * TILE

    def user_side(tile_fn):
        def per_group(group):
            def per_owner(running, owner):
                return running + tile_fn(group, owner), None
            total, _ = lax.scan(per_owner, jnp.zeros((USER_BLK, TILE, RANK), jnp.float32), jnp.arange(N_ITEM, dtype=jnp.int32))
            return total
        return lax.map(per_group, jnp.arange(N_USER, dtype=jnp.int32)).reshape(N_USER * group_rows, RANK)

    def rhs_term(group, owner):
        item_rows = jnp.take(block_grid_height[owner], tile_items[group, owner], axis=0).astype(jnp.float32)
        confidence = confidence_of(tile_values[group, owner]).astype(jnp.float32)
        partial_value = jnp.einsum('tui,tir->tur', confidence, item_rows, precision=highest)
        chosen = chosen_of(tile_users[group, owner], active_all[group, owner], USER_BLK)
        return jnp.einsum('tk,tur->kur', chosen, partial_value, precision=highest)

    def apply_tiles(dir_rows):
        def term(group, owner):
            item_rows = jnp.take(block_grid_height[owner], tile_items[group, owner], axis=0).astype(jnp.float32)
            user_rows = jnp.take(dir_rows[group], tile_users[group, owner], axis=0).astype(jnp.float32)
            scores = jnp.einsum('tur,tir->tui', user_rows, item_rows, precision=highest)
            weighted = (scores * tile_values[group, owner].astype(jnp.float32)).astype(jnp.bfloat16)
            weighted = lax.optimization_barrier(weighted).astype(jnp.float32)
            returned = jnp.einsum('tui,tir->tur', weighted, item_rows, precision=highest)
            chosen = chosen_of(tile_users[group, owner], active_all[group, owner], USER_BLK)
            return jnp.einsum('tk,tur->kur', chosen, returned, precision=highest)
        return user_side(term)

    right_side = user_side(rhs_term)
    solution = jnp.zeros_like(right_side)
    residual = right_side
    direction = right_side
    norm_now = jnp.sum(residual * residual, axis=1, keepdims=True)
    for iteration in range(ITERS):
        dir_rows = direction.astype(jnp.bfloat16).reshape(N_USER, USER_BLK, TILE, RANK)
        image = jnp.dot(direction, item_gram, precision=highest) + apply_tiles(dir_rows)
        step_size = norm_now / (jnp.sum(direction * image, axis=1, keepdims=True) + epsilon)
        solution = solution + step_size * direction
        residual = residual - step_size * image
        norm_next = jnp.sum(residual * residual, axis=1, keepdims=True)
        direction = residual + norm_next / (norm_now + epsilon) * direction
        norm_now = norm_next

    closing_rows = solution.astype(jnp.bfloat16).reshape(N_USER, USER_BLK, TILE, RANK)

    def per_owner(owner):
        def per_group(running, group):
            user_rows = jnp.take(closing_rows[group], tile_users[group, owner], axis=0).astype(jnp.float32)
            confidence = confidence_of(tile_values[group, owner]).astype(jnp.float32)
            partial_value = jnp.einsum('tui,tur->tir', confidence, user_rows, precision=highest)
            chosen = chosen_of(tile_items[group, owner], active_all[group, owner], ITEM_BLK)
            return running + jnp.einsum('tk,tir->kir', chosen, partial_value, precision=highest), None
        total, _ = lax.scan(per_group, jnp.zeros((ITEM_BLK, TILE, RANK), jnp.float32), jnp.arange(N_USER, dtype=jnp.int32))
        return total

    item_rhs = lax.map(per_owner, jnp.arange(N_ITEM, dtype=jnp.int32)).reshape(N_ITEM, ITEM_BLK * TILE, RANK)
    item_rhs = item_rhs * (N_USER * group_rows) ** -0.5
    return solution, item_rhs
```

```python
import functools

import jax
import jax.numpy as jnp
from jax import lax
from jax.experimental import pallas as pl
from jax.experimental.pallas import tpu as pltpu
from jax.sharding import PartitionSpec as P

USER_BLK = 4
ITERS = 3
CHUNK = 256

epsilon = 1e-06
highest = lax.Precision.HIGHEST
MESH = pl.DeviceIdType.MESH
NT = (((1,), (1,)), ((), ()))


def confidence_of(w):
    w = w.astype(jnp.float32)
    return jnp.where(w > 0, 1.0 + w, 0.0).astype(jnp.bfloat16)


def kernel(
    nu, ni, scale,
    inv_ref, y_hbm, gram_hbm, tiles_hbm,
    sol_ref, item_ref,
    tiles, yv, gram, wide, wx, ct, xall, dirs, part, ra, sb, rb,
    load_sem, w_send, w_recv, a_send, a_recv, b_send, b_recv,
    z_send, z_recv, f_send, f_recv, u_send, u_recv, s_send, s_recv,
):
    slots, side, _ = tiles_hbm.shape
    items, rank = yv.shape
    group = wide.shape[0]
    rows = group // ni
    nz = ni // 2
    cols = items // nu
    blocks = items // side
    g, o = lax.axis_index("user"), lax.axis_index("item")
    z, c = lax.div(o, 2), lax.rem(o, 2)
    other = 1 - c
    sib = {"item": z * 2 + other}

    def znum(j):
        return lax.rem(z + (j + nz), nz)

    def unum(j):
        return lax.rem(g + (j + nu), nu)

    def zpeer(j):
        return {"item": znum(j) * 2 + c}

    def upeer(j):
        return {"user": unum(j)}

    def row(zz, cc):
        return pl.ds(pl.multiple_of((zz * 2 + cc) * rows, rows), rows)

    def xrow(gg, zz, cc):
        return pl.ds(pl.multiple_of(gg * group + (zz * 2 + cc) * rows, rows), rows)

    def zrow(zz):
        return pl.ds(pl.multiple_of(zz * rows, rows), rows)

    sent = []

    def rcopy(src, dst, ss, rs, dev):
        return pltpu.make_async_remote_copy(
            src_ref=src, dst_ref=dst, send_sem=ss, recv_sem=rs, device_id=dev, device_id_type=MESH
        )

    def send(*args):
        cp = rcopy(*args)
        cp.start()
        sent.append(cp)

    def arrived(dst, ss, rs, dev):
        rcopy(dst, dst, ss, rs, dev).wait_recv()

    loads = [
        pltpu.make_async_copy(tiles_hbm, tiles.at[pl.ds(0, slots)], load_sem.at[0]),
        pltpu.make_async_copy(y_hbm, yv, load_sem.at[1]),
        pltpu.make_async_copy(gram_hbm, gram, load_sem.at[2]),
    ]
    for cp in loads:
        cp.start()

    barrier = pltpu.get_barrier_semaphore()
    pl.semaphore_signal(barrier, inc=1, device_id=sib, device_id_type=MESH)
    for j in range(1, nz):
        pl.semaphore_signal(barrier, inc=1, device_id=zpeer(j), device_id_type=MESH)
    for j in range(1, nu):
        pl.semaphore_signal(barrier, inc=1, device_id=upeer(j), device_id_type=MESH)

    tiles[slots] = jnp.zeros((side, side), jnp.bfloat16)
    loads[0].wait()
    for u in range(USER_BLK):
        for b in range(blocks):
            wide[u * side : (u + 1) * side, b * side : (b + 1) * side] = tiles[inv_ref[u * blocks + b]]
    for cp in loads[1:]:
        cp.wait()
    pl.semaphore_wait(barrier, nz + nu - 1)

    def wcol(gg):
        return pl.ds(pl.multiple_of(gg * cols, cols), cols)

    for j in range(1, nu):
        send(wide.at[:, wcol(unum(j))], wx.at[j], w_send.at[j], w_recv.at[j], upeer(j))

    def turn(j):
        if j == 0:
            block = wide[:, wcol(g)]
        else:
            arrived(wx.at[j], w_send.at[j], w_recv.at[j], upeer(-j))
            block = wx[j]
        ct[j] = confidence_of(block).T

    turns = [[], [], [], []]
    for j in range(nu):
        turns[j * 4 // nu].append(j)

    def step_of(i):
        return pl.ds(pl.multiple_of(i * CHUNK, CHUNK), CHUNK)

    def rhs_pass():
        part[0] = jnp.zeros((group, rank), jnp.float32)

        def body(i, _):
            at = step_of(i)
            part[0] += jnp.dot(confidence_of(wide[:, at]), yv[at, :], preferred_element_type=jnp.float32)
            return 0

        lax.fori_loop(0, items // CHUNK, body, 0)

    def apply_pass(k):
        part[k] = jnp.zeros((group, rank), jnp.float32)

        def body(i, _):
            at = step_of(i)
            yc = yv[at, :]
            scores = lax.dot_general(dirs[k - 1], yc, NT, preferred_element_type=jnp.float32)
            weighted = (scores * wide[:, at].astype(jnp.float32)).astype(jnp.bfloat16)
            part[k] += jnp.dot(weighted, yc, preferred_element_type=jnp.float32)
            return 0

        lax.fori_loop(0, items // CHUNK, body, 0)

    order = list(range(1, nz)) + [0]

    def reduce_start(k):
        for j in order:
            zz = znum(j)
            send(part.at[k, row(zz, other)], ra.at[k, zrow(zz)], a_send.at[k, j], a_recv.at[k, j], sib)
        own = None
        for j in order:
            zz = znum(j)
            arrived(ra.at[k, zrow(zz)], a_send.at[k, j], a_recv.at[k, j], sib)
            total = part[k, row(zz, c)] + ra[k, zrow(zz)]
            if j:
                sb[k, zrow(zz)] = total.astype(jnp.bfloat16)
                send(sb.at[k, zrow(zz)], rb.at[k, zrow(z)], b_send.at[k, j], b_recv.at[k, j], zpeer(j))
            else:
                own = total
        return own

    def reduce_end(k, own):
        for j in range(1, nz):
            src = zrow(znum(-j))
            arrived(rb.at[k, src], b_send.at[k, j], b_recv.at[k, j], zpeer(-j))
            own = own + rb[k, src].astype(jnp.float32)
        return own

    def gather(k, value, filler):
        buf = dirs.at[k]
        mine = row(z, c)
        buf[mine, :] = value.astype(jnp.bfloat16)
        for j in range(1, nz):
            send(buf.at[mine], buf.at[mine], z_send.at[k, j], z_recv.at[k, j], zpeer(j))
        send(buf.at[mine], buf.at[mine], f_send.at[k, 0], f_recv.at[k, 0], sib)
        filler()
        for j in range(1, nz):
            src = row(znum(-j), c)
            arrived(buf.at[src], z_send.at[k, j], z_recv.at[k, j], zpeer(-j))
            send(buf.at[src], buf.at[src], f_send.at[k, j], f_recv.at[k, j], sib)
        for j in range(nz):
            src = row(znum(-j), other)
            arrived(buf.at[src], f_send.at[k, j], f_recv.at[k, j], sib)

    def nothing():
        pass

    def turn_all(which):
        for j in turns[which]:
            turn(j)

    rhs_pass()
    own = reduce_start(0)
    residual = reduce_end(0, own)
    direction = residual
    sol = jnp.zeros_like(residual)
    norm = jnp.sum(residual * residual, axis=1, keepdims=True)
    for k in range(1, ITERS + 1):
        gather(k - 1, direction, functools.partial(turn_all, 2) if k == ITERS else nothing)
        apply_pass(k)
        own = reduce_start(k)
        image = jnp.dot(direction, gram[...], precision=highest, preferred_element_type=jnp.float32)
        if k == 1:
            turn_all(0)
        elif k == 2:
            turn_all(1)
        elif k == ITERS:
            turn_all(3)
        image = image + reduce_end(k, own)
        alpha = norm / (jnp.sum(direction * image, axis=1, keepdims=True) + epsilon)
        sol = sol + alpha * direction
        if k < ITERS:
            residual = residual - alpha * image
            norm_next = jnp.sum(residual * residual, axis=1, keepdims=True)
            direction = residual + norm_next / (norm + epsilon) * direction
            norm = norm_next

    mine = xrow(g, z, c)
    xall[mine, :] = sol.astype(jnp.bfloat16)
    k = ITERS

    def share(piece, j):
        for v in range(1, nu):
            send(xall.at[piece], xall.at[piece], u_send.at[v, j], u_recv.at[v, j], upeer(v))
        send(xall.at[piece], xall.at[piece], s_send.at[0, j], s_recv.at[0, j], sib)

    for j in range(1, nz):
        send(xall.at[mine], xall.at[mine], z_send.at[k, j], z_recv.at[k, j], zpeer(j))
    share(mine, 0)
    sol_ref[...] = sol
    for j in range(1, nz):
        piece = xrow(g, znum(-j), c)
        arrived(xall.at[piece], z_send.at[k, j], z_recv.at[k, j], zpeer(-j))
        share(piece, j)

    def finish(v):
        src = unum(-v)
        for j in range(nz):
            arrived(xall.at[xrow(src, znum(-j), other)], s_send.at[v, j], s_recv.at[v, j], sib)
        here = pl.ds(pl.multiple_of(src * group, group), group)
        return jnp.dot(ct[v], xall[here, :], preferred_element_type=jnp.float32)

    for v in range(1, nu):
        for j in range(nz):
            piece = xrow(unum(-v), znum(-j), c)
            arrived(xall.at[piece], u_send.at[v, j], u_recv.at[v, j], upeer(-v))
            send(xall.at[piece], xall.at[piece], s_send.at[v, j], s_recv.at[v, j], sib)
        if v == 1:
            item_ref[...] = finish(0)
        else:
            item_ref[...] += finish(v - 1)
    item_ref[...] = (item_ref[...] + finish(nu - 1)) * scale
    for cp in sent:
        cp.wait_send()


def make_local(nu, ni):
    def local(item_factors, item_gram, tile_users, tile_items, tile_counts, tile_values):
        items, rank = item_factors.shape
        slots, side = tile_values.shape[2], tile_values.shape[-1]
        blocks = items // side
        group = USER_BLK * side
        rows = group // ni
        nz = ni // 2
        cols = items // nu
        at = jnp.arange(slots, dtype=jnp.int32)
        key = jnp.where(at < tile_counts[0, 0], tile_users[0, 0] * blocks + tile_items[0, 0], -1)
        match = key[None, :] == jnp.arange(USER_BLK * blocks, dtype=jnp.int32)[:, None]
        inv = slots - jnp.sum(jnp.where(match, slots - at[None, :], 0), axis=1)
        scale = float(nu * group) ** -0.5
        bf, f4 = jnp.bfloat16, jnp.float32
        dma = pltpu.SemaphoreType.DMA
        rounds = ITERS + 1
        anywhere = pl.BlockSpec(memory_space=pl.ANY)
        vmem = pl.BlockSpec(memory_space=pltpu.VMEM)
        sol, item = pl.pallas_call(
            functools.partial(kernel, nu, ni, scale),
            out_shape=(
                jax.ShapeDtypeStruct((rows, rank), f4),
                jax.ShapeDtypeStruct((cols, rank), f4),
            ),
            in_specs=[pl.BlockSpec(memory_space=pltpu.SMEM), anywhere, anywhere, anywhere],
            out_specs=(vmem, vmem),
            scratch_shapes=[
                pltpu.VMEM((slots + 1, side, side), bf),
                pltpu.VMEM((items, rank), bf),
                pltpu.VMEM((rank, rank), f4),
                pltpu.VMEM((group, items), bf),
                pltpu.VMEM((nu, group, cols), bf),
                pltpu.VMEM((nu, cols, group), bf),
                pltpu.VMEM((nu * group, rank), bf),
                pltpu.VMEM((ITERS, group, rank), bf),
                pltpu.VMEM((rounds, group, rank), f4),
                pltpu.VMEM((rounds, nz * rows, rank), f4),
                pltpu.VMEM((rounds, nz * rows, rank), bf),
                pltpu.VMEM((rounds, nz * rows, rank), bf),
                dma((3,)),
                dma((nu,)), dma((nu,)),
                dma((rounds, nz)), dma((rounds, nz)),
                dma((rounds, nz)), dma((rounds, nz)),
                dma((rounds, nz)), dma((rounds, nz)),
                dma((rounds, nz)), dma((rounds, nz)),
                dma((nu, nz)), dma((nu, nz)),
                dma((nu, nz)), dma((nu, nz)),
            ],
            compiler_params=pltpu.CompilerParams(collective_id=0, has_side_effects=True),
        )(inv, item_factors, item_gram, tile_values.reshape(slots, side, side))
        return sol, item[None]

    return local


def solution(mesh):
    return jax.shard_map(
        make_local(mesh.shape["user"], mesh.shape["item"]),
        mesh=mesh,
        in_specs=(
            P("item", None),
            P(),
            P("user", "item", None),
            P("user", "item", None),
            P("user", "item"),
            P("user", "item", None, None, None),
        ),
        out_specs=(P(("user", "item"), None), P("item", "user", None)),
        check_vma=False,
    )
```

```python
import functools

import jax
import jax.numpy as jnp
from jax import lax
from jax.experimental import pallas as pl
from jax.experimental.pallas import tpu as pltpu
from jax.sharding import PartitionSpec as P

USER_BLK = 4
ITERS = 3
CHUNK = 256
STREAMS = 2

epsilon = 1e-06
highest = lax.Precision.HIGHEST
MESH = pl.DeviceIdType.MESH
NT = (((1,), (1,)), ((), ()))


def confidence_of(w):
    w = w.astype(jnp.float32)
    return jnp.where(w > 0, 1.0 + w, 0.0).astype(jnp.bfloat16)


def kernel(
    nu, ni, scale,
    inv_ref, y_hbm, gram_hbm, tiles_hbm,
    sol_ref, item_ref,
    tiles, yv, gram, wide, wx, ct, xall, dirs, part, ra, sb, rb,
    d_state, r_state, x_state, n_state, i_state, sol_in,
    load_sem, w_send, w_recv, a_send, a_recv, b_send, b_recv,
    z_send, z_recv, f_send, f_recv, u_send, u_recv, s_send, s_recv, o_send, o_recv,
):
    slots, side, _ = tiles_hbm.shape
    items, rank = yv.shape
    group = wide.shape[0]
    rows = group // ni
    nz = ni // 2
    owners = nz // STREAMS
    low = (nz - owners) // 2
    stream_rows = group // STREAMS
    cols = items // nu
    blocks = items // side
    g, o = lax.axis_index("user"), lax.axis_index("item")
    z, c = lax.div(o, 2), lax.rem(o, 2)
    other = 1 - c
    sib = {"item": z * 2 + other}
    place = lax.rem(z - low + nz, owners)
    is_owner = (z >= low) & (z < low + owners)

    def znum(j):
        return lax.rem(z + (j + nz), nz)

    def unum(j):
        return lax.rem(g + (j + nu), nu)

    def zpeer(j):
        return {"item": znum(j) * 2 + c}

    def upeer(j):
        return {"user": unum(j)}

    def at_row(s, cc, q, base=0):
        return pl.ds(pl.multiple_of(base + ((s * 2 + cc) * owners + q) * rows, rows), rows)

    def half_rows(s, cc):
        size = owners * rows
        return pl.ds(pl.multiple_of((s * 2 + cc) * size, size), size)

    sent = []

    def rcopy(src, dst, ss, rs, dev):
        return pltpu.make_async_remote_copy(
            src_ref=src, dst_ref=dst, send_sem=ss, recv_sem=rs, device_id=dev, device_id_type=MESH
        )

    def send(*args):
        cp = rcopy(*args)
        cp.start()
        sent.append((None, cp))

    def send_if(cond, *args):
        cp = rcopy(*args)
        pl.when(cond)(cp.start)
        sent.append((cond, cp))

    def arrived(dst, ss, rs, dev):
        rcopy(dst, dst, ss, rs, dev).wait_recv()

    loads = [
        pltpu.make_async_copy(tiles_hbm, tiles.at[pl.ds(0, slots)], load_sem.at[0]),
        pltpu.make_async_copy(y_hbm, yv, load_sem.at[1]),
        pltpu.make_async_copy(gram_hbm, gram, load_sem.at[2]),
    ]
    for cp in loads:
        cp.start()

    barrier = pltpu.get_barrier_semaphore()
    pl.semaphore_signal(barrier, inc=1, device_id=sib, device_id_type=MESH)
    for j in range(1, nz):
        pl.semaphore_signal(barrier, inc=1, device_id=zpeer(j), device_id_type=MESH)
    for j in range(1, nu):
        pl.semaphore_signal(barrier, inc=1, device_id=upeer(j), device_id_type=MESH)

    tiles[slots] = jnp.zeros((side, side), jnp.bfloat16)
    loads[0].wait()
    for b in range(blocks):
        for q in range(owners):
            for s in range(STREAMS):
                for cc in range(2):
                    start = ((q * STREAMS + s) * 2 + cc) * rows
                    to = ((s * 2 + cc) * owners + q) * rows
                    u, off = start // side, start % side
                    wide[to : to + rows, b * side : (b + 1) * side] = tiles[
                        inv_ref[u * blocks + b], off : off + rows, :
                    ]
    for cp in loads[1:]:
        cp.wait()

    def wcol(gg):
        return pl.ds(pl.multiple_of(gg * cols, cols), cols)

    def turn(j):
        if j == 0:
            block = wide[:, wcol(g)]
        else:
            arrived(wx.at[j], w_send.at[j], w_recv.at[j], upeer(-j))
            block = wx[j]
        ct[j] = confidence_of(block).T

    turns = [[], [], [], []]
    for j in range(nu):
        turns[j * 4 // nu].append(j)

    def step_of(i):
        return pl.ds(pl.multiple_of(i * CHUNK, CHUNK), CHUNK)

    def stream_pass(k, s):
        here = slice(s * stream_rows, (s + 1) * stream_rows)

        def body(i, acc):
            at = step_of(i)
            yc = yv[at, :]
            if k == 0:
                weighted = confidence_of(wide[here, at])
            else:
                scores = lax.dot_general(dirs[k - 1, here], yc, NT, preferred_element_type=jnp.float32)
                weighted = (scores * wide[here, at].astype(jnp.float32)).astype(jnp.bfloat16)
            part[k, here] += jnp.dot(weighted, yc, preferred_element_type=jnp.float32)
            return acc

        part[k, here] = jnp.zeros((stream_rows, rank), jnp.float32)
        lax.fori_loop(0, items // CHUNK, body, 0)
        send(part.at[k, half_rows(s, other)], ra.at[k, s], a_send.at[k, s], a_recv.at[k, s], sib)

    def reduce_start(k, s):
        arrived(ra.at[k, s], a_send.at[k, s], a_recv.at[k, s], sib)
        total = part[k, half_rows(s, c)] + ra[k, s]
        ra[k, s] = total
        sb[k, s] = total.astype(jnp.bfloat16)
        for q in range(owners):
            zo = q + low
            j = lax.rem(zo - z + nz, nz)
            piece = sb.at[k, s, pl.ds(q * rows, rows)]
            send_if(
                z != zo, piece, rb.at[k, s, j], b_send.at[k, s, q], b_recv.at[k, s, j], {"item": zo * 2 + c}
            )

    def reduce_end(k, s):
        own = ra[k, s, pl.ds(pl.multiple_of(place * rows, rows), rows)]
        for j in range(1, nz):
            arrived(rb.at[k, s, j], b_send.at[k, s, 0], b_recv.at[k, s, j], zpeer(-j))
            own = own + rb[k, s, j].astype(jnp.float32)
        return own

    def buffer(k):
        return (xall, g * group) if k == ITERS else (dirs.at[k], 0)

    def gather_start(k, s, value):
        buf, base = buffer(k)
        mine = at_row(s, c, place, base)
        buf[mine, :] = value.astype(jnp.bfloat16)

    def gather_send(k, s):
        buf, base = buffer(k)
        mine = at_row(s, c, place, base)
        for j in range(1, nz):
            send_if(
                is_owner, buf.at[mine], buf.at[mine], z_send.at[k, s, j], z_recv.at[k, s, place], zpeer(j)
            )

    def gather_pass(k, s):
        buf, base = buffer(k)
        for q in range(owners):
            zo = q + low
            piece = at_row(s, c, q, base)

            @pl.when(z != zo)
            def _():
                arrived(buf.at[piece], z_send.at[k, s, 0], z_recv.at[k, s, q], {"item": lax.rem(o + 2, ni)})

            if k == ITERS:
                for v in range(1, nu):
                    send(buf.at[piece], buf.at[piece], u_send.at[v, s, q], u_recv.at[v, s, q], upeer(v))
            send(buf.at[piece], buf.at[piece], f_send.at[k, s, q], f_recv.at[k, s, q], sib)

    def gather_end(k, s):
        buf, base = buffer(k)
        for q in range(owners):
            arrived(buf.at[at_row(s, other, q, base)], f_send.at[k, s, q], f_recv.at[k, s, q], sib)

    def turn_all(which):
        for j in turns[which]:
            turn(j)

    def update(k, s):
        total = reduce_end(k, s)
        if k == 0:
            r_state[s] = total
            d_state[s] = total
            x_state[s] = jnp.zeros_like(total)
            n_state[s] = jnp.sum(total * total, axis=1, keepdims=True)
            gather_start(k, s, total)
            return
        direction = d_state[s]
        image = i_state[s] + total
        norm = n_state[s]
        alpha = norm / (jnp.sum(direction * image, axis=1, keepdims=True) + epsilon)
        sol = x_state[s] + alpha * direction
        x_state[s] = sol
        if k == ITERS:
            gather_start(k, s, sol)
            return
        residual = r_state[s] - alpha * image
        r_state[s] = residual
        norm_next = jnp.sum(residual * residual, axis=1, keepdims=True)
        direction = residual + norm_next / (norm + epsilon) * direction
        d_state[s] = direction
        n_state[s] = norm_next
        gather_start(k, s, direction)

    def grams():
        for s in range(STREAMS):
            i_state[s] = jnp.dot(
                d_state[s], gram[...], precision=highest, preferred_element_type=jnp.float32
            )

    for k in range(ITERS + 1):
        for s in range(STREAMS):
            if k:
                gather_end(k - 1, s)
            elif s == 0:
                pl.semaphore_wait(barrier, nz + nu - 1)
            stream_pass(k, s)
        for s in range(STREAMS):
            reduce_start(k, s)
        if k == 0:
            for j in range(1, nu):
                send(wide.at[:, wcol(unum(j))], wx.at[j], w_send.at[j], w_recv.at[j], upeer(j))
        else:
            pl.when(is_owner)(grams)
        if k == 1:
            turn_all(0)
        elif k == 2:
            turn_all(1)
        elif k == ITERS:
            turn_all(2)
            turn_all(3)
        for s in range(STREAMS):
            pl.when(is_owner)(functools.partial(update, k, s))
            gather_send(k, s)
        for s in range(STREAMS):
            gather_pass(k, s)

    k = ITERS
    for q in range(owners):
        for s in range(STREAMS):
            target = q * STREAMS + s
            if target != q + low:
                send_if(
                    z == q + low, x_state.at[s], sol_in, o_send.at[s], o_recv, {"item": target * 2 + c}
                )

    def finish(v):
        src = unum(-v)
        for s in range(STREAMS):
            for q in range(owners):
                piece = xall.at[at_row(s, other, q, src * group)]
                if v:
                    arrived(piece, s_send.at[v, s, q], s_recv.at[v, s, q], sib)
                else:
                    arrived(piece, f_send.at[k, s, q], f_recv.at[k, s, q], sib)
        here = pl.ds(pl.multiple_of(src * group, group), group)
        return jnp.dot(ct[v], xall[here, :], preferred_element_type=jnp.float32)

    for v in range(1, nu):
        for s in range(STREAMS):
            for q in range(owners):
                piece = xall.at[at_row(s, c, q, unum(-v) * group)]
                arrived(piece, u_send.at[v, s, q], u_recv.at[v, s, q], upeer(-v))
                send(piece, piece, s_send.at[v, s, q], s_recv.at[v, s, q], sib)
        if v == 1:
            item_ref[...] = finish(0)
        else:
            item_ref[...] += finish(v - 1)

    for target in range(nz):
        owner = target // STREAMS + low

        @pl.when(z == target)
        def _():
            if owner == target:
                sol_ref[...] = x_state[target % STREAMS]
            else:
                arrived(sol_in, o_send.at[0], o_recv, {"item": owner * 2 + c})
                sol_ref[...] = sol_in[...]

    item_ref[...] = (item_ref[...] + finish(nu - 1)) * scale
    for cond, cp in sent:
        if cond is None:
            cp.wait_send()
        else:
            pl.when(cond)(cp.wait_send)


def make_local(nu, ni):
    def local(item_factors, item_gram, tile_users, tile_items, tile_counts, tile_values):
        items, rank = item_factors.shape
        slots, side = tile_values.shape[2], tile_values.shape[-1]
        blocks = items // side
        group = USER_BLK * side
        rows = group // ni
        nz = ni // 2
        owners = nz // STREAMS
        cols = items // nu
        at = jnp.arange(slots, dtype=jnp.int32)
        key = jnp.where(at < tile_counts[0, 0], tile_users[0, 0] * blocks + tile_items[0, 0], -1)
        match = key[None, :] == jnp.arange(USER_BLK * blocks, dtype=jnp.int32)[:, None]
        inv = slots - jnp.sum(jnp.where(match, slots - at[None, :], 0), axis=1)
        scale = float(nu * group) ** -0.5
        bf, f4 = jnp.bfloat16, jnp.float32
        dma = pltpu.SemaphoreType.DMA
        rounds = ITERS + 1
        anywhere = pl.BlockSpec(memory_space=pl.ANY)
        vmem = pl.BlockSpec(memory_space=pltpu.VMEM)
        sol, item = pl.pallas_call(
            functools.partial(kernel, nu, ni, scale),
            out_shape=(
                jax.ShapeDtypeStruct((rows, rank), f4),
                jax.ShapeDtypeStruct((cols, rank), f4),
            ),
            in_specs=[pl.BlockSpec(memory_space=pltpu.SMEM), anywhere, anywhere, anywhere],
            out_specs=(vmem, vmem),
            scratch_shapes=[
                pltpu.VMEM((slots + 1, side, side), bf),
                pltpu.VMEM((items, rank), bf),
                pltpu.VMEM((rank, rank), f4),
                pltpu.VMEM((group, items), bf),
                pltpu.VMEM((nu, group, cols), bf),
                pltpu.VMEM((nu, cols, group), bf),
                pltpu.VMEM((nu * group, rank), bf),
                pltpu.VMEM((ITERS, group, rank), bf),
                pltpu.VMEM((rounds, group, rank), f4),
                pltpu.VMEM((rounds, STREAMS, owners * rows, rank), f4),
                pltpu.VMEM((rounds, STREAMS, owners * rows, rank), bf),
                pltpu.VMEM((rounds, STREAMS, nz, rows, rank), bf),
                pltpu.VMEM((STREAMS, rows, rank), f4),
                pltpu.VMEM((STREAMS, rows, rank), f4),
                pltpu.VMEM((STREAMS, rows, rank), f4),
                pltpu.VMEM((STREAMS, rows, 1), f4),
                pltpu.VMEM((STREAMS, rows, rank), f4),
                pltpu.VMEM((rows, rank), f4),
                dma((3,)),
                dma((nu,)), dma((nu,)),
                dma((rounds, STREAMS)), dma((rounds, STREAMS)),
                dma((rounds, STREAMS, owners)), dma((rounds, STREAMS, nz)),
                dma((rounds, STREAMS, nz)), dma((rounds, STREAMS, owners)),
                dma((rounds, STREAMS, owners)), dma((rounds, STREAMS, owners)),
                dma((nu, STREAMS, owners)), dma((nu, STREAMS, owners)),
                dma((nu, STREAMS, owners)), dma((nu, STREAMS, owners)),
                dma((STREAMS,)), dma(()),
            ],
            compiler_params=pltpu.CompilerParams(collective_id=0, has_side_effects=True),
        )(inv, item_factors, item_gram, tile_values.reshape(slots, side, side))
        return sol, item[None]

    return local


def solution(mesh):
    return jax.shard_map(
        make_local(mesh.shape["user"], mesh.shape["item"]),
        mesh=mesh,
        in_specs=(
            P("item", None),
            P(),
            P("user", "item", None),
            P("user", "item", None),
            P("user", "item"),
            P("user", "item", None, None, None),
        ),
        out_specs=(P(("user", "item"), None), P("item", "user", None)),
        check_vma=False,
    )
```

```python
import functools

import jax
import jax.numpy as jnp
from jax import lax
from jax.experimental import pallas as pl
from jax.experimental.pallas import tpu as pltpu
from jax.sharding import PartitionSpec as P

USER_BLK = 4
ITERS = 3
CHUNK = 512
STREAMS = 2

epsilon = 1e-06
highest = lax.Precision.HIGHEST
MESH = pl.DeviceIdType.MESH
NT = (((1,), (1,)), ((), ()))


def confidence_of(w):
    w = w.astype(jnp.float32)
    return jnp.where(w > 0, 1.0 + w, 0.0).astype(jnp.bfloat16)


def kernel(
    nu, ni, scale,
    inv_ref, y_hbm, gram_hbm, tiles_hbm,
    sol_ref, item_ref,
    tiles, yv, gram, wide, wx, ct, xall, dirs, part, ra, sb, rb,
    d_state, r_state, x_state, n_state, i_state, sol_in,
    load_sem, w_send, w_recv, a_send, a_recv, b_send, b_recv,
    z_send, z_recv, f_send, f_recv, u_send, u_recv, s_send, s_recv, o_send, o_recv,
):
    slots, side, _ = tiles_hbm.shape
    items, rank = yv.shape
    group = wide.shape[0]
    rows = group // ni
    nz = ni // 2
    owners = nz // STREAMS
    low = (nz - owners) // 2
    stream_rows = group // STREAMS
    cols = items // nu
    blocks = items // side
    g, o = lax.axis_index("user"), lax.axis_index("item")
    z, c = lax.div(o, 2), lax.rem(o, 2)
    other = 1 - c
    sib = {"item": z * 2 + other}
    place = lax.rem(z - low + nz, owners)
    is_owner = (z >= low) & (z < low + owners)

    def znum(j):
        return lax.rem(z + (j + nz), nz)

    def unum(j):
        return lax.rem(g + (j + nu), nu)

    def zpeer(j):
        return {"item": znum(j) * 2 + c}

    def upeer(j):
        return {"user": unum(j)}

    def at_row(s, cc, q, base=0):
        return pl.ds(pl.multiple_of(base + ((s * 2 + cc) * owners + q) * rows, rows), rows)

    def half_rows(s, cc):
        size = owners * rows
        return pl.ds(pl.multiple_of((s * 2 + cc) * size, size), size)

    sent = []

    def rcopy(src, dst, ss, rs, dev):
        return pltpu.make_async_remote_copy(
            src_ref=src, dst_ref=dst, send_sem=ss, recv_sem=rs, device_id=dev, device_id_type=MESH
        )

    def send(*args):
        cp = rcopy(*args)
        cp.start()
        sent.append((None, cp))

    def send_if(cond, *args):
        cp = rcopy(*args)
        pl.when(cond)(cp.start)
        sent.append((cond, cp))

    def arrived(dst, ss, rs, dev):
        rcopy(dst, dst, ss, rs, dev).wait_recv()

    loads = [
        pltpu.make_async_copy(tiles_hbm, tiles.at[pl.ds(0, slots)], load_sem.at[0]),
        pltpu.make_async_copy(y_hbm, yv, load_sem.at[1]),
        pltpu.make_async_copy(gram_hbm, gram, load_sem.at[2]),
    ]
    for cp in loads:
        cp.start()

    barrier = pltpu.get_barrier_semaphore()
    pl.semaphore_signal(barrier, inc=1, device_id=sib, device_id_type=MESH)
    for j in range(1, nz):
        pl.semaphore_signal(barrier, inc=1, device_id=zpeer(j), device_id_type=MESH)
    for j in range(1, nu):
        pl.semaphore_signal(barrier, inc=1, device_id=upeer(j), device_id_type=MESH)

    tiles[slots] = jnp.zeros((side, side), jnp.bfloat16)
    loads[0].wait()
    for b in range(blocks):
        for q in range(owners):
            for s in range(STREAMS):
                for cc in range(2):
                    start = ((q * STREAMS + s) * 2 + cc) * rows
                    to = ((s * 2 + cc) * owners + q) * rows
                    u, off = start // side, start % side
                    wide[to : to + rows, b * side : (b + 1) * side] = tiles[
                        inv_ref[u * blocks + b], off : off + rows, :
                    ]
    for cp in loads[1:]:
        cp.wait()

    def wcol(gg):
        return pl.ds(pl.multiple_of(gg * cols, cols), cols)

    def turn(j):
        if j == 0:
            block = wide[:, wcol(g)]
        else:
            arrived(wx.at[j], w_send.at[j], w_recv.at[j], upeer(-j))
            block = wx[j]
        ct[j] = confidence_of(block).T

    turns = [[], [], [], []]
    for j in range(nu):
        turns[j * 4 // nu].append(j)

    def step_of(i):
        return pl.ds(pl.multiple_of(i * CHUNK, CHUNK), CHUNK)

    def stream_pass(k, s):
        here = slice(s * stream_rows, (s + 1) * stream_rows)

        def body(i, acc):
            at = step_of(i)
            yc = yv[at, :]
            if k == 0:
                weighted = confidence_of(wide[here, at])
            else:
                scores = lax.dot_general(dirs[k - 1, here], yc, NT, preferred_element_type=jnp.float32)
                weighted = (scores * wide[here, at].astype(jnp.float32)).astype(jnp.bfloat16)
            part[k, here] += jnp.dot(weighted, yc, preferred_element_type=jnp.float32)
            return acc

        part[k, here] = jnp.zeros((stream_rows, rank), jnp.float32)
        lax.fori_loop(0, items // CHUNK, body, 0, unroll=4)

    def reduce_start(k, s):
        arrived(ra.at[k, s], a_send.at[k, s], a_recv.at[k, s], sib)
        total = part[k, half_rows(s, c)] + ra[k, s]
        ra[k, s] = total
        sb[k, s] = total.astype(jnp.bfloat16)
        for q in range(owners):
            zo = q + low
            j = lax.rem(zo - z + nz, nz)
            piece = sb.at[k, s, pl.ds(q * rows, rows)]
            send_if(
                z != zo, piece, rb.at[k, s, j], b_send.at[k, s, q], b_recv.at[k, s, j], {"item": zo * 2 + c}
            )

    def reduce_end(k, s):
        own = ra[k, s, pl.ds(pl.multiple_of(place * rows, rows), rows)]
        for j in range(1, nz):
            arrived(rb.at[k, s, j], b_send.at[k, s, 0], b_recv.at[k, s, j], zpeer(-j))
            own = own + rb[k, s, j].astype(jnp.float32)
        return own

    def buffer(k):
        return (xall, g * group) if k == ITERS else (dirs.at[k], 0)

    def gather_start(k, s, value):
        buf, base = buffer(k)
        mine = at_row(s, c, place, base)
        buf[mine, :] = value.astype(jnp.bfloat16)

    def gather_send(k, s):
        buf, base = buffer(k)
        mine = at_row(s, c, place, base)
        for j in range(1, nz):
            send_if(
                is_owner, buf.at[mine], buf.at[mine], z_send.at[k, s, j], z_recv.at[k, s, place], zpeer(j)
            )

    def gather_pass(k, s):
        buf, base = buffer(k)
        for q in range(owners):
            zo = q + low
            piece = at_row(s, c, q, base)

            @pl.when(z != zo)
            def _():
                arrived(buf.at[piece], z_send.at[k, s, 0], z_recv.at[k, s, q], {"item": lax.rem(o + 2, ni)})

            if k == ITERS:
                for v in range(1, nu):
                    send(buf.at[piece], buf.at[piece], u_send.at[v, s, q], u_recv.at[v, s, q], upeer(v))
            send(buf.at[piece], buf.at[piece], f_send.at[k, s, q], f_recv.at[k, s, q], sib)

    def gather_end(k, s):
        buf, base = buffer(k)
        for q in range(owners):
            arrived(buf.at[at_row(s, other, q, base)], f_send.at[k, s, q], f_recv.at[k, s, q], sib)

    def turn_all(which):
        for j in turns[which]:
            turn(j)

    def update(k, s):
        total = reduce_end(k, s)
        if k == 0:
            r_state[s] = total
            d_state[s] = total
            x_state[s] = jnp.zeros_like(total)
            n_state[s] = jnp.sum(total * total, axis=1, keepdims=True)
            gather_start(k, s, total)
            return
        direction = d_state[s]
        image = i_state[s] + total
        norm = n_state[s]
        alpha = norm / (jnp.sum(direction * image, axis=1, keepdims=True) + epsilon)
        sol = x_state[s] + alpha * direction
        x_state[s] = sol
        if k == ITERS:
            gather_start(k, s, sol)
            return
        residual = r_state[s] - alpha * image
        r_state[s] = residual
        norm_next = jnp.sum(residual * residual, axis=1, keepdims=True)
        direction = residual + norm_next / (norm + epsilon) * direction
        d_state[s] = direction
        n_state[s] = norm_next
        gather_start(k, s, direction)

    def grams():
        for s in range(STREAMS):
            i_state[s] = jnp.dot(
                d_state[s], gram[...], precision=highest, preferred_element_type=jnp.float32
            )

    for k in range(ITERS + 1):
        for s in range(STREAMS):
            if k:
                gather_end(k - 1, s)
            stream_pass(k, s)
            if k == 0 and s == 0:
                pl.semaphore_wait(barrier, nz + nu - 1)
            send(part.at[k, half_rows(s, other)], ra.at[k, s], a_send.at[k, s], a_recv.at[k, s], sib)
        for s in range(STREAMS):
            reduce_start(k, s)
        if k == 0:
            for j in range(1, nu):
                send(wide.at[:, wcol(unum(j))], wx.at[j], w_send.at[j], w_recv.at[j], upeer(j))
        else:
            pl.when(is_owner)(grams)
        if k == 1:
            turn_all(0)
        elif k == 2:
            turn_all(1)
        elif k == ITERS:
            turn_all(2)
            turn_all(3)
        for s in range(STREAMS):
            pl.when(is_owner)(functools.partial(update, k, s))
            gather_send(k, s)
        for s in range(STREAMS):
            gather_pass(k, s)

    k = ITERS
    for q in range(owners):
        for s in range(STREAMS):
            target = q * STREAMS + s
            if target != q + low:
                send_if(
                    z == q + low, x_state.at[s], sol_in, o_send.at[s], o_recv, {"item": target * 2 + c}
                )

    def finish(v):
        src = unum(-v)
        for s in range(STREAMS):
            for q in range(owners):
                piece = xall.at[at_row(s, other, q, src * group)]
                if v:
                    arrived(piece, s_send.at[v, s, q], s_recv.at[v, s, q], sib)
                else:
                    arrived(piece, f_send.at[k, s, q], f_recv.at[k, s, q], sib)
        here = pl.ds(pl.multiple_of(src * group, group), group)
        return jnp.dot(ct[v], xall[here, :], preferred_element_type=jnp.float32)

    for v in range(1, nu):
        for s in range(STREAMS):
            for q in range(owners):
                piece = xall.at[at_row(s, c, q, unum(-v) * group)]
                arrived(piece, u_send.at[v, s, q], u_recv.at[v, s, q], upeer(-v))
                send(piece, piece, s_send.at[v, s, q], s_recv.at[v, s, q], sib)
        if v == 1:
            item_ref[...] = finish(0)
        else:
            item_ref[...] += finish(v - 1)

    for target in range(nz):
        owner = target // STREAMS + low

        @pl.when(z == target)
        def _():
            if owner == target:
                sol_ref[...] = x_state[target % STREAMS]
            else:
                arrived(sol_in, o_send.at[0], o_recv, {"item": owner * 2 + c})
                sol_ref[...] = sol_in[...]

    item_ref[...] = (item_ref[...] + finish(nu - 1)) * scale
    for cond, cp in sent:
        if cond is None:
            cp.wait_send()
        else:
            pl.when(cond)(cp.wait_send)


def make_local(nu, ni):
    def local(item_factors, item_gram, tile_users, tile_items, tile_counts, tile_values):
        items, rank = item_factors.shape
        slots, side = tile_values.shape[2], tile_values.shape[-1]
        blocks = items // side
        group = USER_BLK * side
        rows = group // ni
        nz = ni // 2
        owners = nz // STREAMS
        cols = items // nu
        at = jnp.arange(slots, dtype=jnp.int32)
        key = jnp.where(at < tile_counts[0, 0], tile_users[0, 0] * blocks + tile_items[0, 0], -1)
        match = key[None, :] == jnp.arange(USER_BLK * blocks, dtype=jnp.int32)[:, None]
        inv = slots - jnp.sum(jnp.where(match, slots - at[None, :], 0), axis=1)
        scale = float(nu * group) ** -0.5
        bf, f4 = jnp.bfloat16, jnp.float32
        dma = pltpu.SemaphoreType.DMA
        rounds = ITERS + 1
        anywhere = pl.BlockSpec(memory_space=pl.ANY)
        vmem = pl.BlockSpec(memory_space=pltpu.VMEM)
        sol, item = pl.pallas_call(
            functools.partial(kernel, nu, ni, scale),
            out_shape=(
                jax.ShapeDtypeStruct((rows, rank), f4),
                jax.ShapeDtypeStruct((cols, rank), f4),
            ),
            in_specs=[pl.BlockSpec(memory_space=pltpu.SMEM), anywhere, anywhere, anywhere],
            out_specs=(vmem, vmem),
            scratch_shapes=[
                pltpu.VMEM((slots + 1, side, side), bf),
                pltpu.VMEM((items, rank), bf),
                pltpu.VMEM((rank, rank), f4),
                pltpu.VMEM((group, items), bf),
                pltpu.VMEM((nu, group, cols), bf),
                pltpu.VMEM((nu, cols, group), bf),
                pltpu.VMEM((nu * group, rank), bf),
                pltpu.VMEM((ITERS, group, rank), bf),
                pltpu.VMEM((rounds, group, rank), f4),
                pltpu.VMEM((rounds, STREAMS, owners * rows, rank), f4),
                pltpu.VMEM((rounds, STREAMS, owners * rows, rank), bf),
                pltpu.VMEM((rounds, STREAMS, nz, rows, rank), bf),
                pltpu.VMEM((STREAMS, rows, rank), f4),
                pltpu.VMEM((STREAMS, rows, rank), f4),
                pltpu.VMEM((STREAMS, rows, rank), f4),
                pltpu.VMEM((STREAMS, rows, 1), f4),
                pltpu.VMEM((STREAMS, rows, rank), f4),
                pltpu.VMEM((rows, rank), f4),
                dma((3,)),
                dma((nu,)), dma((nu,)),
                dma((rounds, STREAMS)), dma((rounds, STREAMS)),
                dma((rounds, STREAMS, owners)), dma((rounds, STREAMS, nz)),
                dma((rounds, STREAMS, nz)), dma((rounds, STREAMS, owners)),
                dma((rounds, STREAMS, owners)), dma((rounds, STREAMS, owners)),
                dma((nu, STREAMS, owners)), dma((nu, STREAMS, owners)),
                dma((nu, STREAMS, owners)), dma((nu, STREAMS, owners)),
                dma((STREAMS,)), dma(()),
            ],
            compiler_params=pltpu.CompilerParams(collective_id=0, has_side_effects=True),
        )(inv, item_factors, item_gram, tile_values.reshape(slots, side, side))
        return sol, item[None]

    return local


def solution(mesh):
    return jax.shard_map(
        make_local(mesh.shape["user"], mesh.shape["item"]),
        mesh=mesh,
        in_specs=(
            P("item", None),
            P(),
            P("user", "item", None),
            P("user", "item", None),
            P("user", "item"),
            P("user", "item", None, None, None),
        ),
        out_specs=(P(("user", "item"), None), P("item", "user", None)),
        check_vma=False,
    )
```

```python
import functools

import jax
import jax.numpy as jnp
from jax import lax
from jax.experimental import pallas as pl
from jax.experimental.pallas import tpu as pltpu
from jax.sharding import PartitionSpec as P

USER_BLK = 4
ITERS = 3
CHUNK = 512
STREAMS = 2

epsilon = 1e-06
highest = lax.Precision.HIGHEST
MESH = pl.DeviceIdType.MESH
NT = (((1,), (1,)), ((), ()))


def confidence_of(w):
    w = w.astype(jnp.float32)
    return jnp.where(w > 0, 1.0 + w, 0.0).astype(jnp.bfloat16)


def kernel(
    nu, ni, scale,
    inv_ref, y_hbm, gram_hbm, tiles_hbm,
    sol_ref, item_ref,
    tiles, yv, gram, wide, wx, ct, xall, dirs, part, ra, sb, rb,
    d_state, r_state, x_state, n_state, i_state, sol_in,
    load_sem, w_send, w_recv, a_send, a_recv, b_send, b_recv,
    z_send, z_recv, f_send, f_recv, u_send, u_recv, s_send, s_recv, o_send, o_recv,
):
    slots, side, _ = tiles_hbm.shape
    items, rank = yv.shape
    group = wide.shape[0]
    rows = group // ni
    nz = ni // 2
    owners = nz // STREAMS
    low = (nz - owners) // 2
    stream_rows = group // STREAMS
    cols = items // nu
    blocks = items // side
    g, o = lax.axis_index("user"), lax.axis_index("item")
    z, c = lax.div(o, 2), lax.rem(o, 2)
    other = 1 - c
    sib = {"item": z * 2 + other}
    place = lax.rem(z - low + nz, owners)
    is_owner = (z >= low) & (z < low + owners)

    def znum(j):
        return lax.rem(z + (j + nz), nz)

    def unum(j):
        return lax.rem(g + (j + nu), nu)

    def zpeer(j):
        return {"item": znum(j) * 2 + c}

    def upeer(j):
        return {"user": unum(j)}

    def at_row(s, cc, q, base=0):
        return pl.ds(pl.multiple_of(base + ((s * 2 + cc) * owners + q) * rows, rows), rows)

    def half_rows(s, cc):
        size = owners * rows
        return pl.ds(pl.multiple_of((s * 2 + cc) * size, size), size)

    sent = []

    def rcopy(src, dst, ss, rs, dev):
        return pltpu.make_async_remote_copy(
            src_ref=src, dst_ref=dst, send_sem=ss, recv_sem=rs, device_id=dev, device_id_type=MESH
        )

    def send(*args):
        cp = rcopy(*args)
        cp.start()
        sent.append((None, cp))

    def send_if(cond, *args):
        cp = rcopy(*args)
        pl.when(cond)(cp.start)
        sent.append((cond, cp))

    def arrived(dst, ss, rs, dev):
        rcopy(dst, dst, ss, rs, dev).wait_recv()

    loads = [
        pltpu.make_async_copy(tiles_hbm, tiles.at[pl.ds(0, slots)], load_sem.at[0]),
        pltpu.make_async_copy(y_hbm, yv, load_sem.at[1]),
        pltpu.make_async_copy(gram_hbm, gram, load_sem.at[2]),
    ]
    for cp in loads:
        cp.start()

    barrier = pltpu.get_barrier_semaphore()
    pl.semaphore_signal(barrier, inc=1, device_id=sib, device_id_type=MESH)
    for j in range(1, nz):
        pl.semaphore_signal(barrier, inc=1, device_id=zpeer(j), device_id_type=MESH)
    for j in range(1, nu):
        pl.semaphore_signal(barrier, inc=1, device_id=upeer(j), device_id_type=MESH)

    tiles[slots] = jnp.zeros((side, side), jnp.bfloat16)
    loads[0].wait()
    for b in range(blocks):
        for q in range(owners):
            for s in range(STREAMS):
                for cc in range(2):
                    start = ((q * STREAMS + s) * 2 + cc) * rows
                    to = ((s * 2 + cc) * owners + q) * rows
                    u, off = start // side, start % side
                    wide[to : to + rows, b * side : (b + 1) * side] = tiles[
                        inv_ref[u * blocks + b], off : off + rows, :
                    ]
    for cp in loads[1:]:
        cp.wait()

    def wcol(gg):
        return pl.ds(pl.multiple_of(gg * cols, cols), cols)

    def turn(j):
        if j == 0:
            block = wide[:, wcol(g)]
        else:
            arrived(wx.at[j], w_send.at[j], w_recv.at[j], upeer(-j))
            block = wx[j]
        ct[j] = confidence_of(block).T

    turns = [[], [], [], []]
    for j in range(nu):
        turns[j * 4 // nu].append(j)

    def step_of(i):
        return pl.ds(pl.multiple_of(i * CHUNK, CHUNK), CHUNK)

    def stream_pass(k, s):
        here = slice(s * stream_rows, (s + 1) * stream_rows)

        def body(i, acc):
            at = step_of(i)
            yc = yv[at, :]
            if k == 0:
                weighted = confidence_of(wide[here, at])
            else:
                scores = lax.dot_general(dirs[k - 1, here], yc, NT, preferred_element_type=jnp.float32)
                weighted = (scores * wide[here, at].astype(jnp.float32)).astype(jnp.bfloat16)
            part[k, here] += jnp.dot(weighted, yc, preferred_element_type=jnp.float32)
            return acc

        part[k, here] = jnp.zeros((stream_rows, rank), jnp.float32)
        lax.fori_loop(0, items // CHUNK, body, 0, unroll=4)

    def reduce_start(k, s):
        arrived(ra.at[k, s], a_send.at[k, s], a_recv.at[k, s], sib)
        total = part[k, half_rows(s, c)] + ra[k, s]
        ra[k, s] = total
        sb[k, s] = total.astype(jnp.bfloat16)
        for q in range(owners):
            zo = q + low
            j = lax.rem(zo - z + nz, nz)
            piece = sb.at[k, s, pl.ds(q * rows, rows)]
            send_if(
                z != zo, piece, rb.at[k, s, j], b_send.at[k, s, q], b_recv.at[k, s, j], {"item": zo * 2 + c}
            )

    def reduce_end(k, s):
        own = ra[k, s, pl.ds(pl.multiple_of(place * rows, rows), rows)]
        for j in range(1, nz):
            arrived(rb.at[k, s, j], b_send.at[k, s, 0], b_recv.at[k, s, j], zpeer(-j))
            own = own + rb[k, s, j].astype(jnp.float32)
        return own

    def buffer(k):
        return (xall, g * group) if k == ITERS else (dirs.at[k], 0)

    def gather_start(k, s, value):
        buf, base = buffer(k)
        mine = at_row(s, c, place, base)
        buf[mine, :] = value.astype(jnp.bfloat16)

    def gather_send(k, s):
        buf, base = buffer(k)
        mine = at_row(s, c, place, base)
        for j in range(1, nz):
            send_if(
                is_owner, buf.at[mine], buf.at[mine], z_send.at[k, s, j], z_recv.at[k, s, place], zpeer(j)
            )

    def gather_pass(k, s):
        buf, base = buffer(k)
        for q in range(owners):
            zo = q + low
            piece = at_row(s, c, q, base)

            @pl.when(z != zo)
            def _():
                arrived(buf.at[piece], z_send.at[k, s, 0], z_recv.at[k, s, q], {"item": lax.rem(o + 2, ni)})

            if k == ITERS:
                for v in range(1, nu):
                    send(buf.at[piece], buf.at[piece], u_send.at[v, s, q], u_recv.at[v, s, q], upeer(v))
            send(buf.at[piece], buf.at[piece], f_send.at[k, s, q], f_recv.at[k, s, q], sib)

    def gather_end(k, s):
        buf, base = buffer(k)
        for q in range(owners):
            arrived(buf.at[at_row(s, other, q, base)], f_send.at[k, s, q], f_recv.at[k, s, q], sib)

    def turn_all(which):
        for j in turns[which]:
            turn(j)

    def update(k, s):
        total = reduce_end(k, s)
        if k == 0:
            r_state[s] = total
            d_state[s] = total
            x_state[s] = jnp.zeros_like(total)
            n_state[s] = jnp.sum(total * total, axis=1, keepdims=True)
            gather_start(k, s, total)
            return
        direction = d_state[s]
        image = i_state[s] + total
        norm = n_state[s]
        alpha = norm / (jnp.sum(direction * image, axis=1, keepdims=True) + epsilon)
        sol = x_state[s] + alpha * direction
        x_state[s] = sol
        if k == ITERS:
            gather_start(k, s, sol)
            return
        residual = r_state[s] - alpha * image
        r_state[s] = residual
        norm_next = jnp.sum(residual * residual, axis=1, keepdims=True)
        direction = residual + norm_next / (norm + epsilon) * direction
        d_state[s] = direction
        n_state[s] = norm_next
        gather_start(k, s, direction)

    def grams():
        for s in range(STREAMS):
            i_state[s] = jnp.dot(
                d_state[s], gram[...], precision=highest, preferred_element_type=jnp.float32
            )

    for k in range(ITERS + 1):
        for s in range(STREAMS):
            if k:
                gather_end(k - 1, s)
            stream_pass(k, s)
            if k == 0 and s == 0:
                pl.semaphore_wait(barrier, nz + nu - 1)
            send(part.at[k, half_rows(s, other)], ra.at[k, s], a_send.at[k, s], a_recv.at[k, s], sib)
        for s in range(STREAMS):
            reduce_start(k, s)
        if k == 0:
            for j in range(1, nu):
                send(wide.at[:, wcol(unum(j))], wx.at[j], w_send.at[j], w_recv.at[j], upeer(j))
        else:
            pl.when(is_owner)(grams)
        if k == 1:
            turn_all(0)
        elif k == 2:
            turn_all(1)
        elif k == ITERS:
            turn_all(2)
            turn_all(3)
        for s in range(STREAMS):
            pl.when(is_owner)(functools.partial(update, k, s))
            gather_send(k, s)
        for s in range(STREAMS):
            gather_pass(k, s)

    k = ITERS
    for q in range(owners):
        for s in range(STREAMS):
            target = q * STREAMS + s
            if target != q + low:
                send_if(
                    z == q + low, x_state.at[s], sol_in, o_send.at[s], o_recv, {"item": target * 2 + c}
                )

    def finish(v):
        src = unum(-v)
        for s in range(STREAMS):
            for q in range(owners):
                piece = xall.at[at_row(s, other, q, src * group)]
                if v:
                    arrived(piece, s_send.at[v, s, q], s_recv.at[v, s, q], sib)
                else:
                    arrived(piece, f_send.at[k, s, q], f_recv.at[k, s, q], sib)
        here = pl.ds(pl.multiple_of(src * group, group), group)
        return jnp.dot(ct[v], xall[here, :], preferred_element_type=jnp.float32)

    for v in range(1, nu):
        for s in range(STREAMS):
            for q in range(owners):
                piece = xall.at[at_row(s, c, q, unum(-v) * group)]
                arrived(piece, u_send.at[v, s, q], u_recv.at[v, s, q], upeer(-v))
                send(piece, piece, s_send.at[v, s, q], s_recv.at[v, s, q], sib)
        if v == 1:
            item_ref[...] = finish(0)
        else:
            item_ref[...] += finish(v - 1)

    for target in range(nz):
        owner = target // STREAMS + low

        @pl.when(z == target)
        def _():
            if owner == target:
                sol_ref[...] = x_state[target % STREAMS]
            else:
                arrived(sol_in, o_send.at[0], o_recv, {"item": owner * 2 + c})
                sol_ref[...] = sol_in[...]

    item_ref[...] = (item_ref[...] + finish(nu - 1)) * scale
    for cond, cp in sent:
        if cond is None:
            cp.wait_send()
        else:
            pl.when(cond)(cp.wait_send)


def place_outputs(sol_in, item_in, sol_out, item_out):
    sol_out[...] = sol_in[...]
    item_out[...] = item_in[...]


def make_local(nu, ni):
    def local(item_factors, item_gram, tile_users, tile_items, tile_counts, tile_values):
        items, rank = item_factors.shape
        slots, side = tile_values.shape[2], tile_values.shape[-1]
        blocks = items // side
        group = USER_BLK * side
        rows = group // ni
        nz = ni // 2
        owners = nz // STREAMS
        cols = items // nu
        at = jnp.arange(slots, dtype=jnp.int32)
        key = jnp.where(at < tile_counts[0, 0], tile_users[0, 0] * blocks + tile_items[0, 0], -1)
        match = key[None, :] == jnp.arange(USER_BLK * blocks, dtype=jnp.int32)[:, None]
        inv = slots - jnp.sum(jnp.where(match, slots - at[None, :], 0), axis=1)
        scale = float(nu * group) ** -0.5
        bf, f4 = jnp.bfloat16, jnp.float32
        dma = pltpu.SemaphoreType.DMA
        rounds = ITERS + 1
        anywhere = pl.BlockSpec(memory_space=pl.ANY)
        vmem = pl.BlockSpec(memory_space=pltpu.VMEM)
        sol, item = pl.pallas_call(
            functools.partial(kernel, nu, ni, scale),
            out_shape=(
                jax.ShapeDtypeStruct((rows, rank), f4),
                jax.ShapeDtypeStruct((cols, rank), f4),
            ),
            in_specs=[pl.BlockSpec(memory_space=pltpu.SMEM), anywhere, anywhere, anywhere],
            out_specs=(vmem, vmem),
            scratch_shapes=[
                pltpu.VMEM((slots + 1, side, side), bf),
                pltpu.VMEM((items, rank), bf),
                pltpu.VMEM((rank, rank), f4),
                pltpu.VMEM((group, items), bf),
                pltpu.VMEM((nu, group, cols), bf),
                pltpu.VMEM((nu, cols, group), bf),
                pltpu.VMEM((nu * group, rank), bf),
                pltpu.VMEM((ITERS, group, rank), bf),
                pltpu.VMEM((rounds, group, rank), f4),
                pltpu.VMEM((rounds, STREAMS, owners * rows, rank), f4),
                pltpu.VMEM((rounds, STREAMS, owners * rows, rank), bf),
                pltpu.VMEM((rounds, STREAMS, nz, rows, rank), bf),
                pltpu.VMEM((STREAMS, rows, rank), f4),
                pltpu.VMEM((STREAMS, rows, rank), f4),
                pltpu.VMEM((STREAMS, rows, rank), f4),
                pltpu.VMEM((STREAMS, rows, 1), f4),
                pltpu.VMEM((STREAMS, rows, rank), f4),
                pltpu.VMEM((rows, rank), f4),
                dma((3,)),
                dma((nu,)), dma((nu,)),
                dma((rounds, STREAMS)), dma((rounds, STREAMS)),
                dma((rounds, STREAMS, owners)), dma((rounds, STREAMS, nz)),
                dma((rounds, STREAMS, nz)), dma((rounds, STREAMS, owners)),
                dma((rounds, STREAMS, owners)), dma((rounds, STREAMS, owners)),
                dma((nu, STREAMS, owners)), dma((nu, STREAMS, owners)),
                dma((nu, STREAMS, owners)), dma((nu, STREAMS, owners)),
                dma((STREAMS,)), dma(()),
            ],
            compiler_params=pltpu.CompilerParams(collective_id=0, has_side_effects=True),
        )(inv, item_factors, item_gram, tile_values.reshape(slots, side, side))
        sol, item = pl.pallas_call(
            place_outputs,
            out_shape=(
                jax.ShapeDtypeStruct((rows, rank), f4),
                jax.ShapeDtypeStruct((cols, rank), f4),
            ),
            in_specs=[vmem, vmem],
            out_specs=(vmem, vmem),
        )(sol, item)
        return sol, item[None]

    return local


def solution(mesh):
    return jax.shard_map(
        make_local(mesh.shape["user"], mesh.shape["item"]),
        mesh=mesh,
        in_specs=(
            P("item", None),
            P(),
            P("user", "item", None),
            P("user", "item", None),
            P("user", "item"),
            P("user", "item", None, None, None),
        ),
        out_specs=(P(("user", "item"), None), P("item", "user", None)),
        check_vma=False,
    )
```
